256 devices in a mesh: ctx: 16 (over y, x_lo, core), feat: 16 (over x_hi, z).
Axes of the slice: x: 4 (x_hi: 2, x_lo: 2; x = x_hi * 2 + x_lo), y: 4, z: 8, core: 2. Of those that a mesh axis runs over, the one named last changes fastest.
Arguments:
- tokens: bfloat16 [4, 4096, 8192], P(None, 'ctx', 'feat'), may hold values from -128 to 128
- norm_gain: float32 [8192], P('feat'), may hold values from 0.1 to 1.9
- qkv_weight: bfloat16 [3, 32, 6, 256, 256], P(None, 'feat'), may hold values from -1 to 1
- out_weight: bfloat16 [32, 6, 256, 256], P('feat'), may hold values from -0.15625 to 0.15625
- section_bits: int32 [5], replicated, may hold values from 0 to 4, each once
- positions: int32 [4, 4096], P(None, 'ctx'), may hold values from 0 to 128, as said below
Outputs:
- layer_out: float32 [4, 4096, 8192], P(None, 'ctx', 'feat')
The draws below stay inside these ranges and needn't reach their ends.
Inputs may be any that keep to these rules, and one draw needn't show every extreme that they name: Within a document, positions rise by one from token to token until they reach 128, where they stay; a document starts at position 0, except the first of a sequence, which may start above 0.
All inputs are finite; a program needn't handle non-finite values.
Results may differ from the reference program's by a relative error of at most 0.0064.
Values may be sent and summed in bfloat16 or wider, within the bound.
No kernel may reach another device: no remote copies, remote signals or barrier semaphores. Data moves between devices by JAX's collectives and lax.ppermute only.
A program may use at most 128 MiB of HBM per device.

```python
import jax
import jax.numpy as jnp
from jax import lax

D = 8192
HEADS = 64
BLOCK = 256
SECTIONS = 5
WINDOW = 128
SEQS = 4
TOK_DEV = 256
NB = 32
HEAD = 128
SEQ_LEN = 4096


def draw_tokens(key, part):
    key_col, key_base = jax.random.split(jax.random.fold_in(key, 11), 2)
    column = jnp.exp(jax.random.uniform(key_col, (D,), jnp.float32, -0.7, 0.7))
    column = column * 3.0 ** (jnp.arange(D, dtype=jnp.float32) / D)
    values = jax.random.truncated_normal(key_base, -4.0, 4.0, (SEQS, SEQ_LEN, D), jnp.float32) * column
    return values.astype(jnp.bfloat16)


def draw_qkv_weight(key, part):
    fan = (SECTIONS + 1) * BLOCK
    shape = (3, NB, SECTIONS + 1, BLOCK, BLOCK)
    values = jax.random.truncated_normal(jax.random.fold_in(key, 23), -4.0, 4.0, shape, jnp.float32) * fan ** (-0.5)
    values = jnp.clip(values, -1.0, 1.0)
    return values.astype(jnp.bfloat16)


def draw_positions(key, part):
    key_start, key_offset = jax.random.split(jax.random.fold_in(key, 37))
    index = jnp.arange(SEQ_LEN, dtype=jnp.int32)
    starts = jax.random.randint(key_start, (SEQS, SEQ_LEN), 0, 3 * TOK_DEV) == 0
    starts = starts & (index > WINDOW)[None, :]
    starts = starts | (index == 0)[None, :]
    latest = lax.cummax(jnp.where(starts, index[None, :], 0), axis=1)
    offset = jax.random.randint(key_offset, (SEQS, 1), 0, 2 * WINDOW)
    raw = index[None, :] - latest + jnp.where(latest == 0, offset, 0)
    return jnp.minimum(raw, WINDOW).astype(jnp.int32)


def level_of(key, extent, pieces, smallest, top_value):
    level = 1.0
    for axis_at, shards_of in pieces:
        draws = jax.random.uniform(jax.random.fold_in(jax.random.fold_in(key, 6), axis_at), (shards_of,), jnp.float32, smallest / len(pieces), top_value / len(pieces))
        level = level * jnp.repeat(jnp.exp(draws), extent[axis_at] // shards_of).reshape((-1,) + (1,) * (len(extent) - 1 - axis_at))
    return level


def centred(key, shape, scale, limit, pieces=(), kind=jnp.bfloat16):
    values = jax.random.normal(key, shape, jnp.float32) * scale
    if len(pieces) > 0:
        values = level_of(key, shape, pieces, -0.22, 0.18) * values
    return jnp.clip(values, min=-limit, max=limit).astype(kind)


def setup_inputs(seed: int = 0) -> dict:
    seeds = jax.random.split(jax.random.key(seed), 7)
    return {
        "tokens": draw_tokens(jax.random.fold_in(seeds[6], 71), 0),
        "norm_gain": jnp.clip(1.0 + 0.18 * jax.random.normal(seeds[1], (D,), jnp.float32), 0.1, 1.9),
        "qkv_weight": draw_qkv_weight(jax.random.fold_in(seeds[6], 71), 0),
        "out_weight": centred(seeds[3], (NB, SECTIONS + 1, BLOCK, BLOCK), ((SECTIONS + 1) * BLOCK) ** -0.5, 0.15625, ((0, 16),)),
        "section_bits": jax.random.permutation(seeds[4], SECTIONS).astype(jnp.int32),
        "positions": draw_positions(jax.random.fold_in(seeds[6], 71), 0),
    }


def apply_butterfly(blocks, weight, section_bits):
    index = jnp.arange(NB, dtype=jnp.int32)
    total = jnp.einsum('rnk,nkj->rnj', blocks.astype(jnp.float32), weight[:, 0].astype(jnp.float32))
    for section in range(1, SECTIONS + 1):
        flip = jnp.left_shift(jnp.int32(1), section_bits[section - 1].astype(jnp.int32))
        partner = jnp.bitwise_xor(index, flip).astype(jnp.int32)
        moved = jnp.take(blocks, partner, axis=1)
        total = total + jnp.einsum('rnk,nkj->rnj', moved.astype(jnp.float32), weight[:, section].astype(jnp.float32))
    return total

def reference(tokens, norm_gain, qkv_weight, out_weight, section_bits, positions):
    seqs, length, width = tokens.shape
    x_full = tokens.astype(jnp.float32)
    mean_sq = lax.optimization_barrier(jnp.mean(x_full * x_full, axis=-1, keepdims=True))
    normed = (x_full * lax.rsqrt(mean_sq + 1e-05) * norm_gain).astype(jnp.bfloat16)
    blocks = normed.reshape(seqs * length, NB, BLOCK)
    projected = []
    for matrix in range(3):
        part = apply_butterfly(blocks, qkv_weight[matrix], section_bits).astype(jnp.bfloat16)
        projected.append(part.reshape(seqs, length, HEADS, HEAD))
    query, keys, values = projected
    keys_pad = jnp.pad(keys, ((0, 0), (WINDOW, 0), (0, 0), (0, 0)))
    values_pad = jnp.pad(values, ((0, 0), (WINDOW, 0), (0, 0), (0, 0)))
    scale = HEAD ** (-0.5)

    def one_block(cidx):
        start = cidx * WINDOW
        qblock = lax.dynamic_slice_in_dim(query, start, WINDOW, 1)
        kblock = lax.dynamic_slice_in_dim(keys_pad, start, 2 * WINDOW, 1)
        vblock = lax.dynamic_slice_in_dim(values_pad, start, 2 * WINDOW, 1)
        pblock = lax.dynamic_slice_in_dim(positions, start, WINDOW, 1)
        scores = jnp.einsum('sqhd,skhd->shqk', qblock.astype(jnp.float32), kblock.astype(jnp.float32)) * scale
        qpos = jnp.arange(WINDOW, dtype=jnp.int32)
        kpos = jnp.arange(2 * WINDOW, dtype=jnp.int32)
        dist = qpos[:, None] + WINDOW - kpos[None, :]
        key_index = start + kpos - WINDOW
        valid = (dist >= 0) & (dist < WINDOW) & (key_index >= 0)[None, :]
        valid = valid[None] & (dist[None] <= pblock[:, :, None])
        masked = jnp.where(valid[:, None], scores, -1e+30)
        top = lax.optimization_barrier(jnp.max(masked, axis=-1, keepdims=True))
        expo = jnp.exp(masked - top)
        weights = (expo / lax.optimization_barrier(jnp.sum(expo, axis=-1, keepdims=True))).astype(jnp.bfloat16)
        mixed = jnp.einsum('shqk,skhd->sqhd', weights.astype(jnp.float32), vblock.astype(jnp.float32))
        return mixed.astype(jnp.bfloat16)
    attended = lax.map(one_block, jnp.arange(length // WINDOW, dtype=jnp.int32))
    attended = jnp.transpose(attended, (1, 0, 2, 3, 4)).reshape(seqs * length, NB, BLOCK)
    projected_out = apply_butterfly(attended, out_weight, section_bits).reshape(seqs, length, width)
    return x_full + projected_out
```

```python
import functools

import jax
import jax.numpy as jnp
from jax import lax
from jax.experimental import pallas as pl
from jax.experimental.pallas import tpu as pltpu
from jax.sharding import PartitionSpec as P

D = 8192
WINDOW = 128
HEAD = 128
LOG2E = 1.4426950408889634


def swapped(value, mask):
    pairs = [(source, source ^ mask) for source in range(lax.axis_size("feat"))]
    return lax.ppermute(value, "feat", pairs)


def passed_along(shard, axis, by):
    devices = lax.axis_size(axis)
    pairs = [(i, i + by) for i in range(devices) if 0 <= i + by < devices]
    return lax.ppermute(shard, axis, pairs)


def section_of(bits_ref, bit):
    section = jnp.int32(0)
    for s in range(bits_ref.shape[0]):
        section = section + jnp.where(bits_ref[s] == bit, jnp.int32(s + 1), jnp.int32(0))
    return section


def gathered(own, partners, l, block):
    cut = lambda ref, j: ref[:, j * block : (j + 1) * block]
    pieces = [cut(own, l), cut(own, 1 - l)] + [cut(p, l) for p in partners]
    return jnp.concatenate(pieces, axis=1)


def stacked(w_ref, lead, sections):
    return jnp.concatenate([w_ref[lead + (s,)] for s in sections], axis=0)


def qkv_kernel(half, bits_ref, ss_ref, ss2_ref, own, p1, p2, p4, p8, w_ref, q_ref, k_ref, v_ref, tail_ref):
    rows = own.shape[0]
    block = w_ref.shape[-1]
    sections = [0] + [section_of(bits_ref, b) for b in range(5)]
    seq = 2 * half + pl.program_id(0)
    sums = ss_ref[pl.ds(seq, 1), :] + ss2_ref[pl.ds(seq, 1), :]
    scale = lax.rsqrt(sums * (1.0 / D) + 1e-05)
    scale = jnp.transpose(jnp.broadcast_to(scale, (128, rows)))
    scale = jnp.concatenate([scale] * (block // 128), axis=1)
    for l in range(2):
        lhs = gathered(own, (p1, p2, p4, p8), l, block)
        for m in range(3):
            rhs = stacked(w_ref, (m, l), sections)
            acc = jnp.dot(lhs, rhs, preferred_element_type=jnp.float32)
            if m == 0:
                value = (acc * (scale * (LOG2E * HEAD**-0.5))).astype(jnp.bfloat16)
                q_ref[:, l * block : (l + 1) * block] = value
            else:
                value = (acc * scale).astype(jnp.bfloat16)
                ref = k_ref if m == 1 else v_ref
                ref[:, l * block : (l + 1) * block] = value
                tail_ref[m - 1, :, l * block : (l + 1) * block] = value[rows - WINDOW :]


def attention_kernel(half, first_ref, pos_ref, q_ref, k_ref, v_ref, rim_ref, out_ref):
    rows, width = q_ref.shape
    seq = 2 * half + pl.program_id(0)
    pos_all = pos_ref[pl.ds(seq, 1), :].astype(jnp.float32)
    shape = (WINDOW, 2 * WINDOW)
    dist = (
        lax.broadcasted_iota(jnp.int32, shape, 0)
        + WINDOW
        - lax.broadcasted_iota(jnp.int32, shape, 1)
    )
    column = lax.broadcasted_iota(jnp.int32, shape, 1)
    window = (dist >= 0) & (dist < WINDOW)
    for c in range(rows // WINDOW):
        pos = jnp.broadcast_to(pos_all[:, c * WINDOW : (c + 1) * WINDOW], (WINDOW, WINDOW))
        pos = jnp.transpose(pos)
        pos = jnp.concatenate([pos, pos], axis=1)
        valid = window & (dist.astype(jnp.float32) <= pos)
        if c == 0:
            valid = valid & (column >= first_ref[0])
        for h in range(width // HEAD):
            cols = slice(h * HEAD, (h + 1) * HEAD)
            query = q_ref[c * WINDOW : (c + 1) * WINDOW, cols]
            if c == 0:
                keys = jnp.concatenate([rim_ref[0, :, cols], k_ref[:WINDOW, cols]], axis=0)
                values = jnp.concatenate([rim_ref[1, :, cols], v_ref[:WINDOW, cols]], axis=0)
            else:
                keys = k_ref[(c - 1) * WINDOW : (c + 1) * WINDOW, cols]
                values = v_ref[(c - 1) * WINDOW : (c + 1) * WINDOW, cols]
            scores = lax.dot_general(
                query, keys, (((1,), (1,)), ((), ())), preferred_element_type=jnp.float32
            )
            scores = jnp.where(valid, scores, -1e30)
            top = jnp.max(scores, axis=-1, keepdims=True)
            expo = jnp.exp2(scores - top)
            total = jnp.sum(expo, axis=-1, keepdims=True)
            mixed = jnp.dot(expo.astype(jnp.bfloat16), values, preferred_element_type=jnp.float32)
            out_ref[c * WINDOW : (c + 1) * WINDOW, cols] = (mixed / total).astype(jnp.bfloat16)


def out_kernel(bits_ref, x_ref, own, p1, p2, p4, p8, w_ref, *rest):
    out_ref = rest[-1]
    block = w_ref.shape[-1]
    sections = [0] + [section_of(bits_ref, b) for b in range(5)]
    for l in range(2):
        lhs = gathered(own, (p1, p2, p4, p8), l, block)
        acc = jnp.dot(lhs, stacked(w_ref, (l,), sections), preferred_element_type=jnp.float32)
        cols = slice(l * block, (l + 1) * block)
        out_ref[:, cols] = x_ref[:, cols].astype(jnp.float32) + acc


SMEM = pl.BlockSpec(memory_space=pltpu.SMEM)
PARAMS = pltpu.CompilerParams(vmem_limit_bytes=48 << 20)


def whole(array):
    return pl.BlockSpec(array.shape, lambda i, n=array.ndim: (0,) * n, pipeline_mode=pl.Buffered(1))


def project(half, bits, sums, own, partners, weight):
    count, rows, width = own.shape
    tile = pl.BlockSpec((None, rows, width), lambda i: (i, 0, 0))
    kind = jax.ShapeDtypeStruct(own.shape, jnp.bfloat16)
    tail = jax.ShapeDtypeStruct((2, count, WINDOW, width), jnp.bfloat16)
    return pl.pallas_call(
        functools.partial(qkv_kernel, half),
        grid=(count,),
        in_specs=[SMEM, whole(sums[0]), whole(sums[1])] + [tile] * 5 + [whole(weight)],
        out_specs=[tile] * 3 + [pl.BlockSpec((2, None, WINDOW, width), lambda i: (0, i, 0, 0))],
        out_shape=[kind, kind, kind, tail],
        compiler_params=PARAMS,
        cost_estimate=pl.CostEstimate(
            flops=2 * 18 * own.size * 256, bytes_accessed=10 * own.size * 2 + weight.size * 2, transcendentals=0
        ),
        name="project",
    )(bits, sums[0], sums[1], own, *partners, weight)


def attend(half, first, positions, query, keys, values, rim):
    count, rows, width = query.shape
    tile = pl.BlockSpec((None, rows, width), lambda i: (i, 0, 0))
    return pl.pallas_call(
        functools.partial(attention_kernel, half),
        grid=(count,),
        in_specs=[SMEM, whole(positions)]
        + [tile] * 3
        + [pl.BlockSpec((2, None, WINDOW, width), lambda i: (0, i, 0, 0))],
        out_specs=tile,
        out_shape=jax.ShapeDtypeStruct(query.shape, jnp.bfloat16),
        compiler_params=PARAMS,
        cost_estimate=pl.CostEstimate(
            flops=query.size * 1024, bytes_accessed=10 * query.size, transcendentals=2 * query.size
        ),
        name="attend",
    )(first, positions, query, keys, values, rim)


def finish(half, bits, tokens, own, partners, weight, earlier):
    count, rows, width = own.shape
    tile = pl.BlockSpec((None, rows, width), lambda i: (i, 0, 0))
    place = pl.BlockSpec((None, rows, width), lambda i: (i + half * count, 0, 0))
    extra = [] if earlier is None else [earlier]
    return pl.pallas_call(
        out_kernel,
        grid=(count,),
        in_specs=[SMEM, place] + [tile] * 5 + [whole(weight)] + [pl.BlockSpec(memory_space=pl.ANY)] * len(extra),
        out_specs=place,
        out_shape=jax.ShapeDtypeStruct(tokens.shape, jnp.float32),
        input_output_aliases={8: 0} if extra else {},
        compiler_params=PARAMS,
        cost_estimate=pl.CostEstimate(
            flops=2 * 6 * own.size * 256, bytes_accessed=16 * own.size + weight.size * 2, transcendentals=0
        ),
        name="finish",
    )(bits, tokens, own, *partners, weight, *extra)


def after(value, *others):
    return lax.optimization_barrier((value,) + others)[0]


def per_device(tokens, norm_gain, qkv_weight, out_weight, section_bits, positions):
    seqs, tok_rows, width = tokens.shape
    x_full = tokens.astype(jnp.float32)
    scaled = (x_full * norm_gain).astype(jnp.bfloat16)
    own = [scaled[:2], scaled[2:]]
    sums = jnp.sum(x_full * x_full, axis=-1)
    first = jnp.where(lax.axis_index("ctx") == 0, WINDOW, 0).astype(jnp.int32)[None]

    z2, z1, x8, z4 = [None] * 2, [None] * 2, [None] * 2, [None] * 2
    z2[0] = swapped(own[0], 2)
    z1[0] = swapped(own[0], 1)
    x8[0] = swapped(own[0], 8)
    other = swapped(sums, 8)
    for mask in (1, 2, 4):
        sums = sums + other
        other = swapped(sums, mask)
    pair = (sums, other)
    later = after(own[1], z2[0])
    z4[0] = swapped(z2[0], 6)
    z2[1] = swapped(later, 2)
    x8[1] = swapped(later, 8)
    latest = after(own[1], z2[1])
    z4[1] = swapped(z2[1], 6)
    z1[1] = swapped(latest, 1)

    mixed = []
    for half in range(2):
        query, keys, values, tail = project(
            half, section_bits, pair, own[half], (z1[half], z2[half], z4[half], x8[half]), qkv_weight
        )
        rim = passed_along(tail, "ctx", 1)
        mixed.append(attend(half, first, positions, query, keys, values, rim))

    z2[0] = swapped(mixed[0], 2)
    z1[0] = swapped(mixed[0], 1)
    x8[0] = swapped(mixed[0], 8)
    z4[0] = swapped(z2[0], 6)
    later = after(mixed[1], z2[0])
    z2[1] = swapped(later, 2)
    x8[1] = swapped(later, 8)
    latest = after(mixed[1], z2[1])
    z4[1] = swapped(z2[1], 6)
    z1[1] = swapped(latest, 1)
    result = None
    for half in range(2):
        result = finish(
            half, section_bits, tokens, mixed[half], (z1[half], z2[half], z4[half], x8[half]), out_weight, result
        )
    return result


def solution(mesh):
    in_specs = (
        P(None, "ctx", "feat"),
        P("feat"),
        P(None, "feat", None, None, None),
        P("feat", None, None, None),
        P(),
        P(None, "ctx"),
    )
    out_specs = P(None, "ctx", "feat")
    return jax.shard_map(
        per_device, mesh=mesh, in_specs=in_specs, out_specs=out_specs, check_vma=False
    )
```

```python
import functools

import jax
import jax.numpy as jnp
from jax import lax
from jax.experimental import pallas as pl
from jax.experimental.pallas import tpu as pltpu
from jax.sharding import PartitionSpec as P


D = 8192
WINDOW = 128
HEAD = 128
SEQS = 4
LOG2E = 1.4426950408889634


def swapped(value, mask):
    pairs = [(source, source ^ mask) for source in range(lax.axis_size("feat"))]
    return lax.ppermute(value, "feat", pairs)


def passed_along(shard, axis, by):
    devices = lax.axis_size(axis)
    pairs = [(i, i + by) for i in range(devices) if 0 <= i + by < devices]
    return lax.ppermute(shard, axis, pairs)


def section_of(bits_ref, bit):
    section = jnp.int32(0)
    for s in range(bits_ref.shape[0]):
        section = section + jnp.where(bits_ref[s] == bit, jnp.int32(s + 1), jnp.int32(0))
    return section


def gathered(refs, l, block):
    cut = lambda pair, j: pair[0][pair[1], :, j * block : (j + 1) * block]
    pieces = [cut(refs[0], l), cut(refs[0], 1 - l)] + [cut(p, l) for p in refs[1:]]
    return jnp.concatenate(pieces, axis=1)


def stacked(w_ref, lead, sections):
    return jnp.concatenate([w_ref[lead + (s,)] for s in sections], axis=0)


def qkv_kernel(seq, bits_ref, s0, s1, s2, s3, own, p1, p2, p4, p8, w_ref, q_ref, k_ref, v_ref, tail_ref):
    rows = own.shape[1]
    block = w_ref.shape[-1]
    sections = [0] + [section_of(bits_ref, b) for b in range(5)]
    row = slice(seq, seq + 1)
    sums = (s0[row, :] + s1[row, :]) + (s2[row, :] + s3[row, :])
    scale = lax.rsqrt(sums * (1.0 / D) + 1e-05)
    scale = jnp.transpose(jnp.broadcast_to(scale, (128, rows)))
    scale = jnp.concatenate([scale] * (block // 128), axis=1)
    for l in range(2):
        lhs = gathered(((own, seq), (p1, 0), (p2, 0), (p4, 0), (p8, seq)), l, block)
        cols = slice(l * block, (l + 1) * block)
        for m in range(3):
            rhs = stacked(w_ref, (m, l), sections)
            acc = jnp.dot(lhs, rhs, preferred_element_type=jnp.float32)
            if m == 0:
                q_ref[:, cols] = (acc * (scale * (LOG2E * HEAD**-0.5))).astype(jnp.bfloat16)
            else:
                value = (acc * scale).astype(jnp.bfloat16)
                ref = k_ref if m == 1 else v_ref
                ref[:, cols] = value
                tail_ref[m - 1, :, cols] = value[rows - WINDOW :]


def attention_kernel(seq, first_ref, pos_ref, q_ref, k_ref, v_ref, rim_ref, out_ref):
    rows, width = q_ref.shape
    pos_all = pos_ref[seq : seq + 1, :].astype(jnp.float32)
    shape = (WINDOW, 2 * WINDOW)
    dist = (
        lax.broadcasted_iota(jnp.int32, shape, 0)
        + WINDOW
        - lax.broadcasted_iota(jnp.int32, shape, 1)
    )
    column = lax.broadcasted_iota(jnp.int32, shape, 1)
    window = (dist >= 0) & (dist < WINDOW)
    for c in range(rows // WINDOW):
        pos = jnp.broadcast_to(pos_all[:, c * WINDOW : (c + 1) * WINDOW], (WINDOW, WINDOW))
        pos = jnp.transpose(pos)
        pos = jnp.concatenate([pos, pos], axis=1)
        valid = window & (dist.astype(jnp.float32) <= pos)
        if c == 0:
            valid = valid & (column >= first_ref[0])
        for h in range(width // HEAD):
            cols = slice(h * HEAD, (h + 1) * HEAD)
            query = q_ref[c * WINDOW : (c + 1) * WINDOW, cols]
            if c == 0:
                keys = jnp.concatenate([rim_ref[0, :, cols], k_ref[:WINDOW, cols]], axis=0)
                values = jnp.concatenate([rim_ref[1, :, cols], v_ref[:WINDOW, cols]], axis=0)
            else:
                keys = k_ref[(c - 1) * WINDOW : (c + 1) * WINDOW, cols]
                values = v_ref[(c - 1) * WINDOW : (c + 1) * WINDOW, cols]
            scores = lax.dot_general(
                query, keys, (((1,), (1,)), ((), ())), preferred_element_type=jnp.float32
            )
            scores = jnp.where(valid, scores, -1e30)
            top = jnp.max(scores, axis=-1, keepdims=True)
            expo = jnp.exp2(scores - top)
            total = jnp.sum(expo, axis=-1, keepdims=True)
            mixed = jnp.dot(expo.astype(jnp.bfloat16), values, preferred_element_type=jnp.float32)
            out_ref[0, c * WINDOW : (c + 1) * WINDOW, cols] = (mixed / total).astype(jnp.bfloat16)


def out_kernel(seq, bits_ref, x_ref, own, p1, p2, p4, p8, w_ref, *rest):
    out_ref = rest[-1]
    block = w_ref.shape[-1]
    sections = [0] + [section_of(bits_ref, b) for b in range(5)]
    for l in range(2):
        lhs = gathered([(p, 0) for p in (own, p1, p2, p4, p8)], l, block)
        acc = jnp.dot(lhs, stacked(w_ref, (l,), sections), preferred_element_type=jnp.float32)
        cols = slice(l * block, (l + 1) * block)
        out_ref[:, cols] = x_ref[seq, :, cols].astype(jnp.float32) + acc


SMEM = pl.BlockSpec(memory_space=pltpu.SMEM)
VMEM = pl.BlockSpec(memory_space=pltpu.VMEM)
PARAMS = pltpu.CompilerParams(vmem_limit_bytes=6 << 20)


def load_kernel(source, target, sem):
    copy = pltpu.make_async_copy(source, target, sem)
    copy.start()
    copy.wait()


def loaded(weight):
    return pl.pallas_call(
        load_kernel,
        in_specs=[pl.BlockSpec(memory_space=pltpu.HBM)],
        out_specs=VMEM,
        out_shape=jax.ShapeDtypeStruct(weight.shape, weight.dtype),
        scratch_shapes=[pltpu.SemaphoreType.DMA],
        compiler_params=PARAMS,
        cost_estimate=pl.CostEstimate(flops=0, bytes_accessed=4 * weight.size, transcendentals=0),
        name="load",
    )(weight)


def project(seq, bits, sums, own, partners, across, weight):
    rows, width = own.shape[1:]
    kind = jax.ShapeDtypeStruct((rows, width), jnp.bfloat16)
    tail = jax.ShapeDtypeStruct((2, WINDOW, width), jnp.bfloat16)
    return pl.pallas_call(
        functools.partial(qkv_kernel, seq),
        in_specs=[SMEM] + [VMEM] * 10,
        out_specs=[VMEM] * 4,
        out_shape=[kind, kind, kind, tail],
        compiler_params=PARAMS,
        cost_estimate=pl.CostEstimate(
            flops=36 * rows * width * 256, bytes_accessed=20 * rows * width, transcendentals=0
        ),
        name="project",
    )(bits, *sums, own, *partners, across, weight)


def attend(seq, first, positions, query, keys, values, rim):
    return pl.pallas_call(
        functools.partial(attention_kernel, seq),
        in_specs=[SMEM] + [VMEM] * 5,
        out_specs=VMEM,
        out_shape=jax.ShapeDtypeStruct((1,) + query.shape, jnp.bfloat16),
        compiler_params=PARAMS,
        cost_estimate=pl.CostEstimate(
            flops=query.size * 1024, bytes_accessed=10 * query.size, transcendentals=2 * query.size
        ),
        name="attend",
    )(first, positions, query, keys, values, rim)


def finish(seq, bits, tokens, own, partners, weight, earlier):
    rows, width = own.shape[1:]
    extra = [] if earlier is None else [earlier]
    return pl.pallas_call(
        functools.partial(out_kernel, seq),
        grid=(1,),
        in_specs=[SMEM] + [VMEM] * 7 + [pl.BlockSpec(memory_space=pl.ANY)] * len(extra),
        out_specs=pl.BlockSpec((None, rows, width), lambda i: (seq, 0, 0)),
        out_shape=jax.ShapeDtypeStruct(tokens.shape, jnp.float32),
        input_output_aliases={8: 0} if extra else {},
        compiler_params=PARAMS,
        cost_estimate=pl.CostEstimate(
            flops=12 * own.size * 256, bytes_accessed=16 * own.size, transcendentals=0
        ),
        name="finish",
    )(bits, tokens, own, *partners, weight, *extra)


def layer(tokens, norm_gain, qkv_weight, out_weight, section_bits, positions):
    x_full = tokens.astype(jnp.float32)
    scaled = (x_full * norm_gain).astype(jnp.bfloat16)
    own = [scaled[c : c + 1] for c in range(SEQS)]
    sums = jnp.sum(x_full * x_full, axis=-1)
    first = jnp.where(lax.axis_index("ctx") == 0, jnp.int32(WINDOW), jnp.int32(0))[None]
    qkv_weight = loaded(qkv_weight)

    z2 = [swapped(own[c], 2) for c in range(SEQS)]
    z1 = [swapped(own[c], 1) for c in range(SEQS)]
    z6 = [swapped(z2[c], 6) for c in range(SEQS)]
    x8 = swapped(scaled, 8)
    near = [swapped(sums, mask) for mask in (1, 8, 9)]
    group = sums + near[0] + near[1] + near[2]
    far = [swapped(group, mask) for mask in (2, 4, 6)]

    mixed = []
    for c in range(SEQS):
        query, keys, values, tail = project(
            c, section_bits, (group, *far), scaled, (z1[c], z2[c], z6[c]), x8, qkv_weight
        )
        rim = passed_along(tail, "ctx", 1)
        mixed.append(attend(c, first, positions, query, keys, values, rim))

    result = None
    for c in range(SEQS):
        y2 = swapped(mixed[c], 2)
        y1 = swapped(mixed[c], 1)
        y8 = swapped(mixed[c], 8)
        y6 = swapped(y2, 6)
        result = finish(c, section_bits, tokens, mixed[c], (y1, y2, y6, y8), out_weight, result)
    return result


def solution(mesh):
    in_specs = (
        P(None, "ctx", "feat"),
        P("feat"),
        P(None, "feat", None, None, None),
        P("feat", None, None, None),
        P(),
        P(None, "ctx"),
    )
    out_specs = P(None, "ctx", "feat")
    return jax.shard_map(layer, mesh=mesh, in_specs=in_specs, out_specs=out_specs, check_vma=False)
```

```python
import functools

import jax
import jax.numpy as jnp
from jax import lax
from jax.experimental import pallas as pl
from jax.experimental.pallas import tpu as pltpu
from jax.sharding import PartitionSpec as P


D = 8192
WINDOW = 128
HEAD = 128
SEQS = 4
LOG2E = 1.4426950408889634

Z1 = ("0", "1", "23",)


def swapped(value, mask):
    pairs = [(source, source ^ mask) for source in range(lax.axis_size("feat"))]
    return lax.ppermute(value, "feat", pairs)


INNER = (1, 2, 5, 6)


def crossed(value, mask, inner):
    ends = range(lax.axis_size("feat"))
    pairs = [(s, s ^ mask) for s in ends if (s % 8 in INNER) == inner]
    return lax.ppermute(value, "feat", pairs)


def passed_along(shard, axis, by):
    devices = lax.axis_size(axis)
    pairs = [(i, i + by) for i in range(devices) if 0 <= i + by < devices]
    return lax.ppermute(shard, axis, pairs)


def section_of(bits_ref, bit):
    section = jnp.int32(0)
    for s in range(bits_ref.shape[0]):
        section = section + jnp.where(bits_ref[s] == bit, jnp.int32(s + 1), jnp.int32(0))
    return section


def gathered(refs, l, block):
    rows = refs[0][0].shape[1]
    cut = lambda pair, j: pair[0][pair[1], :rows, j * block : (j + 1) * block]
    pieces = [cut(refs[0], l), cut(refs[0], 1 - l)] + [cut(p, l) for p in refs[1:]]
    return jnp.concatenate(pieces, axis=1)


def stacked(w_ref, lead, sections):
    return jnp.concatenate([w_ref[lead + (s,)] for s in sections], axis=0)


def split(sums):
    high = sums.astype(jnp.bfloat16)
    low = (sums - high.astype(jnp.float32)).astype(jnp.bfloat16)
    return jnp.concatenate([high, low], axis=1)


def joined(pair):
    half = pair.shape[1] // 2
    return pair[:, :half].astype(jnp.float32) + pair[:, half:].astype(jnp.float32)


def pack_kernel(own, s0, s1, s2, s3, message, total):
    rows = own.shape[1]
    sums = (s0[...] + s1[...]) + (s2[...] + s3[...])
    total[...] = sums
    message[0, :rows] = own[0]
    spare = jnp.zeros((8 - SEQS, sums.shape[1]), jnp.float32)
    message[0, rows:] = split(jnp.concatenate([sums, spare], axis=0))


def repack_kernel(came, s0, message, total):
    rows = s0.shape[1]
    sums = s0[...] + joined(came[0, rows:])[:SEQS]
    total[...] = sums
    message[0, :rows] = came[0, :rows]
    spare = jnp.zeros((8 - SEQS, sums.shape[1]), jnp.float32)
    message[0, rows:] = split(jnp.concatenate([sums, spare], axis=0))


def qkv_kernel(seq, at1, bits_ref, s0, last, own, p1, p2, p4, p8, w_ref, q_ref, k_ref, v_ref, tail_ref):
    rows = own.shape[1]
    block = w_ref.shape[-1]
    sections = [0] + [section_of(bits_ref, b) for b in range(5)]
    sums = (s0[...] + joined(last[0, rows:])[:SEQS])[seq : seq + 1]
    scale = lax.rsqrt(sums * (1.0 / D) + 1e-05)
    scale = jnp.transpose(jnp.broadcast_to(scale, (128, rows)))
    scale = jnp.concatenate([scale] * (block // 128), axis=1)
    for l in range(2):
        lhs = gathered(((own, seq), (p1, at1), (p2, 0), (p4, 0), (p8, seq)), l, block)
        cols = slice(l * block, (l + 1) * block)
        for m in range(3):
            rhs = stacked(w_ref, (m, l), sections)
            acc = jnp.dot(lhs, rhs, preferred_element_type=jnp.float32)
            if m == 0:
                q_ref[:, cols] = (acc * (scale * (LOG2E * HEAD**-0.5))).astype(jnp.bfloat16)
            else:
                value = (acc * scale).astype(jnp.bfloat16)
                ref = k_ref if m == 1 else v_ref
                ref[:, cols] = value
                tail_ref[m - 1, :, cols] = value[rows - WINDOW :]


def attention_kernel(seq, first_ref, pos_ref, q_ref, k_ref, v_ref, rim_ref, out_ref):
    rows, width = q_ref.shape
    pos_all = pos_ref[seq : seq + 1, :].astype(jnp.float32)
    shape = (WINDOW, 2 * WINDOW)
    dist = (
        lax.broadcasted_iota(jnp.int32, shape, 0)
        + WINDOW
        - lax.broadcasted_iota(jnp.int32, shape, 1)
    )
    column = lax.broadcasted_iota(jnp.int32, shape, 1)
    window = (dist >= 0) & (dist < WINDOW)
    for c in range(rows // WINDOW):
        pos = jnp.broadcast_to(pos_all[:, c * WINDOW : (c + 1) * WINDOW], (WINDOW, WINDOW))
        pos = jnp.transpose(pos)
        pos = jnp.concatenate([pos, pos], axis=1)
        valid = window & (dist.astype(jnp.float32) <= pos)
        if c == 0:
            valid = valid & (column >= first_ref[0])
        for h in range(width // HEAD):
            cols = slice(h * HEAD, (h + 1) * HEAD)
            query = q_ref[c * WINDOW : (c + 1) * WINDOW, cols]
            if c == 0:
                keys = jnp.concatenate([rim_ref[0, :, cols], k_ref[:WINDOW, cols]], axis=0)
                values = jnp.concatenate([rim_ref[1, :, cols], v_ref[:WINDOW, cols]], axis=0)
            else:
                keys = k_ref[(c - 1) * WINDOW : (c + 1) * WINDOW, cols]
                values = v_ref[(c - 1) * WINDOW : (c + 1) * WINDOW, cols]
            scores = lax.dot_general(
                query, keys, (((1,), (1,)), ((), ())), preferred_element_type=jnp.float32
            )
            scores = jnp.where(valid, scores, -1e30)
            top = jnp.max(scores, axis=-1, keepdims=True)
            expo = jnp.exp2(scores - top)
            total = jnp.sum(expo, axis=-1, keepdims=True)
            mixed = jnp.dot(expo.astype(jnp.bfloat16), values, preferred_element_type=jnp.float32)
            out_ref[0, c * WINDOW : (c + 1) * WINDOW, cols] = (mixed / total).astype(jnp.bfloat16)


def pick_kernel(bits_ref, w_ref, out_ref):
    for i in range(2):
        section = section_of(bits_ref, 2 + i)
        for l in range(2):
            out_ref[l, i] = w_ref[l, section]


def partial_kernel(p4, p2, w_ref, out_ref):
    block = w_ref.shape[-1]
    for l in range(2):
        cols = slice(l * block, (l + 1) * block)
        lhs = jnp.concatenate([p4[0, :, cols], p2[0, :, cols]], axis=1)
        acc = jnp.dot(lhs, stacked(w_ref, (l,), (0, 1)), preferred_element_type=jnp.float32)
        out_ref[0, :, cols] = acc.astype(jnp.bfloat16)


def out_kernel(seq, bits_ref, x_ref, own, p1, p2, p4, p8, add, w_ref, *rest):
    out_ref = rest[-1]
    block = w_ref.shape[-1]
    sections = [0] + [section_of(bits_ref, b) for b in range(5)]
    for l in range(2):
        lhs = gathered([(p, 0) for p in (own, p1, p2, p4, p8)], l, block)
        acc = jnp.dot(lhs, stacked(w_ref, (l,), sections), preferred_element_type=jnp.float32)
        cols = slice(l * block, (l + 1) * block)
        base = x_ref[seq, :, cols].astype(jnp.float32) + add[0, :, cols].astype(jnp.float32)
        out_ref[:, cols] = base + acc


SMEM = pl.BlockSpec(memory_space=pltpu.SMEM)
VMEM = pl.BlockSpec(memory_space=pltpu.VMEM)
PARAMS = pltpu.CompilerParams(vmem_limit_bytes=6 << 20)


def load_kernel(source, target, sem):
    copy = pltpu.make_async_copy(source, target, sem)
    copy.start()
    copy.wait()


def loaded(weight):
    return pl.pallas_call(
        load_kernel,
        in_specs=[pl.BlockSpec(memory_space=pltpu.HBM)],
        out_specs=VMEM,
        out_shape=jax.ShapeDtypeStruct(weight.shape, weight.dtype),
        scratch_shapes=[pltpu.SemaphoreType.DMA],
        compiler_params=PARAMS,
        cost_estimate=pl.CostEstimate(flops=0, bytes_accessed=4 * weight.size, transcendentals=0),
        name="load",
    )(weight)


def pack(body, value, *sums):
    rows, width = sums[0].shape[1], value.shape[2]
    return pl.pallas_call(
        body,
        in_specs=[VMEM] * (1 + len(sums)),
        out_specs=[VMEM] * 2,
        out_shape=[
            jax.ShapeDtypeStruct((1, rows + 8, width), jnp.bfloat16),
            jax.ShapeDtypeStruct(sums[0].shape, jnp.float32),
        ],
        compiler_params=PARAMS,
        cost_estimate=pl.CostEstimate(flops=0, bytes_accessed=4 * rows * width, transcendentals=0),
        name="pack",
    )(value, *sums)


def project(seq, at1, bits, sums, own, partners, across, weight):
    rows, width = own.shape[1:]
    kind = jax.ShapeDtypeStruct((rows, width), jnp.bfloat16)
    tail = jax.ShapeDtypeStruct((2, WINDOW, width), jnp.bfloat16)
    return pl.pallas_call(
        functools.partial(qkv_kernel, seq, at1),
        in_specs=[SMEM] + [VMEM] * 8,
        out_specs=[VMEM] * 4,
        out_shape=[kind, kind, kind, tail],
        compiler_params=PARAMS,
        cost_estimate=pl.CostEstimate(
            flops=36 * rows * width * 256, bytes_accessed=20 * rows * width, transcendentals=0
        ),
        name="project",
    )(bits, *sums, own, *partners, across, weight)


def attend(seq, first, positions, query, keys, values, rim):
    return pl.pallas_call(
        functools.partial(attention_kernel, seq),
        in_specs=[SMEM] + [VMEM] * 5,
        out_specs=VMEM,
        out_shape=jax.ShapeDtypeStruct((1,) + query.shape, jnp.bfloat16),
        compiler_params=PARAMS,
        cost_estimate=pl.CostEstimate(
            flops=query.size * 1024, bytes_accessed=10 * query.size, transcendentals=2 * query.size
        ),
        name="attend",
    )(first, positions, query, keys, values, rim)


def picked(bits, weight):
    _, _, block, width = weight.shape
    return pl.pallas_call(
        pick_kernel,
        in_specs=[SMEM, VMEM],
        out_specs=VMEM,
        out_shape=jax.ShapeDtypeStruct((2, 2, block, width), weight.dtype),
        compiler_params=PARAMS,
        cost_estimate=pl.CostEstimate(flops=0, bytes_accessed=16 * block * width, transcendentals=0),
        name="pick",
    )(bits, weight)


def partial(far, near, weight):
    return pl.pallas_call(
        partial_kernel,
        in_specs=[VMEM] * 3,
        out_specs=VMEM,
        out_shape=jax.ShapeDtypeStruct(far.shape, jnp.bfloat16),
        compiler_params=PARAMS,
        cost_estimate=pl.CostEstimate(
            flops=4 * far.size * 256, bytes_accessed=6 * far.size, transcendentals=0
        ),
        name="partial",
    )(far, near, weight)


def finish(seq, bits, tokens, own, partners, weight, earlier):
    rows, width = own.shape[1:]
    extra = [] if earlier is None else [earlier]
    return pl.pallas_call(
        functools.partial(out_kernel, seq),
        grid=(1,),
        in_specs=[SMEM] + [VMEM] * 8 + [pl.BlockSpec(memory_space=pl.ANY)] * len(extra),
        out_specs=pl.BlockSpec((None, rows, width), lambda i: (seq, 0, 0)),
        out_shape=jax.ShapeDtypeStruct(tokens.shape, jnp.float32),
        input_output_aliases={9: 0} if extra else {},
        compiler_params=PARAMS,
        cost_estimate=pl.CostEstimate(
            flops=12 * own.size * 256, bytes_accessed=16 * own.size, transcendentals=0
        ),
        name="finish",
    )(bits, tokens, own, *partners, weight, *extra)


def layer(tokens, norm_gain, qkv_weight, out_weight, section_bits, positions):
    x_full = tokens.astype(jnp.float32)
    scaled = (x_full * norm_gain).astype(jnp.bfloat16)
    own = [scaled[c : c + 1] for c in range(SEQS)]
    sums = jnp.sum(x_full * x_full, axis=-1)
    first = jnp.where(lax.axis_index("ctx") == 0, jnp.int32(WINDOW), jnp.int32(0))[None]
    qkv_weight = loaded(qkv_weight)

    near = [swapped(sums, mask) for mask in (1, 8, 9)]
    packed, group = pack(pack_kernel, own[0], sums, *near)
    z2 = [swapped(packed if c == 0 else own[c], 2) for c in range(SEQS)]
    relayed, group = pack(repack_kernel, z2[0], group)
    z2[0] = relayed
    z6 = [swapped(z2[c], 6) for c in range(SEQS)]
    z1 = {}
    for name in Z1:
        lo, hi = int(name[0]), int(name[-1]) + 1
        part = swapped(own[lo] if hi == lo + 1 else scaled[lo:hi], 1)
        for c in range(lo, hi):
            z1[c] = (part, c - lo)
    x8 = swapped(scaled, 8)

    mixed = []
    for c in range(SEQS):
        query, keys, values, tail = project(
            c, z1[c][1], section_bits, (group, z6[0]), scaled, (z1[c][0], z2[c], z6[c]), x8, qkv_weight
        )
        rim = passed_along(tail, "ctx", 1)
        mixed.append(attend(c, first, positions, query, keys, values, rim))

    part = picked(section_bits, out_weight)
    outer_weight = crossed(part, 6, False)
    result = None
    for c in range(SEQS):
        own = mixed[c]
        y1 = swapped(own, 1)
        y8 = swapped(own, 8)
        y2 = crossed(y1, 3, True)
        y4 = crossed(y1, 5, False)
        both = partial(y4, y2, outer_weight)
        add = crossed(both, 6, True)
        result = finish(
            c, section_bits, tokens, own, (y1, y2, y4, y8, add), out_weight, result
        )
    return result


def solution(mesh):
    in_specs = (
        P(None, "ctx", "feat"),
        P("feat"),
        P(None, "feat", None, None, None),
        P("feat", None, None, None),
        P(),
        P(None, "ctx"),
    )
    out_specs = P(None, "ctx", "feat")
    return jax.shard_map(layer, mesh=mesh, in_specs=in_specs, out_specs=out_specs, check_vma=False)
```

```python
import functools

import jax
import jax.numpy as jnp
from jax import lax
from jax.experimental import pallas as pl
from jax.experimental.pallas import tpu as pltpu
from jax.sharding import PartitionSpec as P


D = 8192
WINDOW = 128
HEAD = 128
SEQS = 4
LOG2E = 1.4426950408889634

Z1 = ("0", "1", "23",)


def swapped(value, mask):
    pairs = [(source, source ^ mask) for source in range(lax.axis_size("feat"))]
    return lax.ppermute(value, "feat", pairs)


def passed_along(shard, axis, by):
    devices = lax.axis_size(axis)
    pairs = [(i, i + by) for i in range(devices) if 0 <= i + by < devices]
    return lax.ppermute(shard, axis, pairs)


def section_of(bits_ref, bit):
    section = jnp.int32(0)
    for s in range(bits_ref.shape[0]):
        section = section + jnp.where(bits_ref[s] == bit, jnp.int32(s + 1), jnp.int32(0))
    return section


def gathered(refs, l, block):
    rows = refs[0][0].shape[1]
    cut = lambda pair, j: pair[0][pair[1], :rows, j * block : (j + 1) * block]
    pieces = [cut(refs[0], l), cut(refs[0], 1 - l)] + [cut(p, l) for p in refs[1:]]
    return jnp.concatenate(pieces, axis=1)


def stacked(w_ref, lead, sections):
    return jnp.concatenate([w_ref[lead + (s,)] for s in sections], axis=0)


def split(sums):
    high = sums.astype(jnp.bfloat16)
    low = (sums - high.astype(jnp.float32)).astype(jnp.bfloat16)
    return jnp.concatenate([high, low], axis=1)


def joined(pair):
    half = pair.shape[1] // 2
    return pair[:, :half].astype(jnp.float32) + pair[:, half:].astype(jnp.float32)


def pack_kernel(own, s0, s1, s2, s3, message, total):
    rows = own.shape[1]
    sums = (s0[...] + s1[...]) + (s2[...] + s3[...])
    total[...] = sums
    message[0, :rows] = own[0]
    spare = jnp.zeros((8 - SEQS, sums.shape[1]), jnp.float32)
    message[0, rows:] = split(jnp.concatenate([sums, spare], axis=0))


def repack_kernel(came, s0, message, total):
    rows = s0.shape[1]
    sums = s0[...] + joined(came[0, rows:])[:SEQS]
    total[...] = sums
    message[0, :rows] = came[0, :rows]
    spare = jnp.zeros((8 - SEQS, sums.shape[1]), jnp.float32)
    message[0, rows:] = split(jnp.concatenate([sums, spare], axis=0))


def qkv_kernel(seq, at1, bits_ref, s0, last, own, p1, p2, p4, p8, w_ref, q_ref, k_ref, v_ref, tail_ref):
    rows = own.shape[1]
    block = w_ref.shape[-1]
    sections = [0] + [section_of(bits_ref, b) for b in range(5)]
    sums = (s0[...] + joined(last[0, rows:])[:SEQS])[seq : seq + 1]
    scale = lax.rsqrt(sums * (1.0 / D) + 1e-05)
    scale = jnp.transpose(jnp.broadcast_to(scale, (128, rows)))
    scale = jnp.concatenate([scale] * (block // 128), axis=1)
    for l in range(2):
        lhs = gathered(((own, seq), (p1, at1), (p2, 0), (p4, 0), (p8, seq)), l, block)
        cols = slice(l * block, (l + 1) * block)
        for m in range(3):
            rhs = stacked(w_ref, (m, l), sections)
            acc = jnp.dot(lhs, rhs, preferred_element_type=jnp.float32)
            if m == 0:
                q_ref[:, cols] = (acc * (scale * (LOG2E * HEAD**-0.5))).astype(jnp.bfloat16)
            else:
                value = (acc * scale).astype(jnp.bfloat16)
                ref = k_ref if m == 1 else v_ref
                ref[:, cols] = value
                tail_ref[m - 1, :, cols] = value[rows - WINDOW :]


def attention_kernel(seq, first_ref, pos_ref, q_ref, k_ref, v_ref, rim_ref, out_ref):
    rows, width = q_ref.shape
    pos_all = pos_ref[seq : seq + 1, :].astype(jnp.float32)
    shape = (WINDOW, 2 * WINDOW)
    dist = (
        lax.broadcasted_iota(jnp.int32, shape, 0)
        + WINDOW
        - lax.broadcasted_iota(jnp.int32, shape, 1)
    )
    column = lax.broadcasted_iota(jnp.int32, shape, 1)
    window = (dist >= 0) & (dist < WINDOW)
    for c in range(rows // WINDOW):
        pos = jnp.broadcast_to(pos_all[:, c * WINDOW : (c + 1) * WINDOW], (WINDOW, WINDOW))
        pos = jnp.transpose(pos)
        pos = jnp.concatenate([pos, pos], axis=1)
        valid = window & (dist.astype(jnp.float32) <= pos)
        if c == 0:
            valid = valid & (column >= first_ref[0])
        for h in range(width // HEAD):
            cols = slice(h * HEAD, (h + 1) * HEAD)
            query = q_ref[c * WINDOW : (c + 1) * WINDOW, cols]
            if c == 0:
                keys = jnp.concatenate([rim_ref[0, :, cols], k_ref[:WINDOW, cols]], axis=0)
                values = jnp.concatenate([rim_ref[1, :, cols], v_ref[:WINDOW, cols]], axis=0)
            else:
                keys = k_ref[(c - 1) * WINDOW : (c + 1) * WINDOW, cols]
                values = v_ref[(c - 1) * WINDOW : (c + 1) * WINDOW, cols]
            scores = lax.dot_general(
                query, keys, (((1,), (1,)), ((), ())), preferred_element_type=jnp.float32
            )
            scores = jnp.where(valid, scores, -1e30)
            top = jnp.max(scores, axis=-1, keepdims=True)
            expo = jnp.exp2(scores - top)
            total = jnp.sum(expo, axis=-1, keepdims=True)
            mixed = jnp.dot(expo.astype(jnp.bfloat16), values, preferred_element_type=jnp.float32)
            out_ref[0, c * WINDOW : (c + 1) * WINDOW, cols] = (mixed / total).astype(jnp.bfloat16)


def out_kernel(seq, bits_ref, x_ref, own, p1, p2, p4, p8, w_ref, *rest):
    out_ref = rest[-1]
    block = w_ref.shape[-1]
    sections = [0] + [section_of(bits_ref, b) for b in range(5)]
    for l in range(2):
        lhs = gathered([(p, 0) for p in (own, p1, p2, p4, p8)], l, block)
        acc = jnp.dot(lhs, stacked(w_ref, (l,), sections), preferred_element_type=jnp.float32)
        cols = slice(l * block, (l + 1) * block)
        out_ref[:, cols] = x_ref[seq, :, cols].astype(jnp.float32) + acc


SMEM = pl.BlockSpec(memory_space=pltpu.SMEM)
VMEM = pl.BlockSpec(memory_space=pltpu.VMEM)
PARAMS = pltpu.CompilerParams(vmem_limit_bytes=6 << 20)


def load_kernel(source, target, sem):
    copy = pltpu.make_async_copy(source, target, sem)
    copy.start()
    copy.wait()


def loaded(weight):
    return pl.pallas_call(
        load_kernel,
        in_specs=[pl.BlockSpec(memory_space=pltpu.HBM)],
        out_specs=VMEM,
        out_shape=jax.ShapeDtypeStruct(weight.shape, weight.dtype),
        scratch_shapes=[pltpu.SemaphoreType.DMA],
        compiler_params=PARAMS,
        cost_estimate=pl.CostEstimate(flops=0, bytes_accessed=4 * weight.size, transcendentals=0),
        name="load",
    )(weight)


def pack(body, value, *sums):
    rows, width = sums[0].shape[1], value.shape[2]
    return pl.pallas_call(
        body,
        in_specs=[VMEM] * (1 + len(sums)),
        out_specs=[VMEM] * 2,
        out_shape=[
            jax.ShapeDtypeStruct((1, rows + 8, width), jnp.bfloat16),
            jax.ShapeDtypeStruct(sums[0].shape, jnp.float32),
        ],
        compiler_params=PARAMS,
        cost_estimate=pl.CostEstimate(flops=0, bytes_accessed=4 * rows * width, transcendentals=0),
        name="pack",
    )(value, *sums)


def project(seq, at1, bits, sums, own, partners, across, weight):
    rows, width = own.shape[1:]
    kind = jax.ShapeDtypeStruct((rows, width), jnp.bfloat16)
    tail = jax.ShapeDtypeStruct((2, WINDOW, width), jnp.bfloat16)
    return pl.pallas_call(
        functools.partial(qkv_kernel, seq, at1),
        in_specs=[SMEM] + [VMEM] * 8,
        out_specs=[VMEM] * 4,
        out_shape=[kind, kind, kind, tail],
        compiler_params=PARAMS,
        cost_estimate=pl.CostEstimate(
            flops=36 * rows * width * 256, bytes_accessed=20 * rows * width, transcendentals=0
        ),
        name="project",
    )(bits, *sums, own, *partners, across, weight)


def attend(seq, first, positions, query, keys, values, rim):
    return pl.pallas_call(
        functools.partial(attention_kernel, seq),
        in_specs=[SMEM] + [VMEM] * 5,
        out_specs=VMEM,
        out_shape=jax.ShapeDtypeStruct((1,) + query.shape, jnp.bfloat16),
        compiler_params=PARAMS,
        cost_estimate=pl.CostEstimate(
            flops=query.size * 1024, bytes_accessed=10 * query.size, transcendentals=2 * query.size
        ),
        name="attend",
    )(first, positions, query, keys, values, rim)


def finish(seq, bits, tokens, own, partners, weight, earlier):
    rows, width = own.shape[1:]
    extra = [] if earlier is None else [earlier]
    return pl.pallas_call(
        functools.partial(out_kernel, seq),
        grid=(1,),
        in_specs=[SMEM] + [VMEM] * 7 + [pl.BlockSpec(memory_space=pl.ANY)] * len(extra),
        out_specs=pl.BlockSpec((None, rows, width), lambda i: (seq, 0, 0)),
        out_shape=jax.ShapeDtypeStruct(tokens.shape, jnp.float32),
        input_output_aliases={8: 0} if extra else {},
        compiler_params=PARAMS,
        cost_estimate=pl.CostEstimate(
            flops=12 * own.size * 256, bytes_accessed=16 * own.size, transcendentals=0
        ),
        name="finish",
    )(bits, tokens, own, *partners, weight, *extra)


def layer(tokens, norm_gain, qkv_weight, out_weight, section_bits, positions):
    x_full = tokens.astype(jnp.float32)
    scaled = (x_full * norm_gain).astype(jnp.bfloat16)
    own = [scaled[c : c + 1] for c in range(SEQS)]
    sums = jnp.sum(x_full * x_full, axis=-1)
    first = jnp.where(lax.axis_index("ctx") == 0, jnp.int32(WINDOW), jnp.int32(0))[None]
    qkv_weight = loaded(qkv_weight)

    near = [swapped(sums, mask) for mask in (1, 8, 9)]
    packed, group = pack(pack_kernel, own[0], sums, *near)
    z2 = [swapped(packed if c == 0 else own[c], 2) for c in range(SEQS)]
    relayed, group = pack(repack_kernel, z2[0], group)
    z2[0] = relayed
    z6 = [swapped(z2[c], 6) for c in range(SEQS)]
    z1 = {}
    for name in Z1:
        lo, hi = int(name[0]), int(name[-1]) + 1
        part = swapped(own[lo] if hi == lo + 1 else scaled[lo:hi], 1)
        for c in range(lo, hi):
            z1[c] = (part, c - lo)
    x8 = swapped(scaled, 8)

    mixed = []
    for c in range(SEQS):
        query, keys, values, tail = project(
            c, z1[c][1], section_bits, (group, z6[0]), scaled, (z1[c][0], z2[c], z6[c]), x8, qkv_weight
        )
        rim = passed_along(tail, "ctx", 1)
        mixed.append(attend(c, first, positions, query, keys, values, rim))

    result = None
    for c in range(SEQS):
        y2 = swapped(mixed[c], 2)
        y1 = swapped(mixed[c], 1)
        y8 = swapped(mixed[c], 8)
        y6 = swapped(y2, 6)
        result = finish(c, section_bits, tokens, mixed[c], (y1, y2, y6, y8), out_weight, result)
    return result


def solution(mesh):
    in_specs = (
        P(None, "ctx", "feat"),
        P("feat"),
        P(None, "feat", None, None, None),
        P("feat", None, None, None),
        P(),
        P(None, "ctx"),
    )
    out_specs = P(None, "ctx", "feat")
    return jax.shard_map(layer, mesh=mesh, in_specs=in_specs, out_specs=out_specs, check_vma=False)
```
